32 devices in a mesh: row: 8 (over z, y), col: 4 (over x, core).
Axes of the slice: x: 2, y: 2, z: 4, core: 2. Of those that a mesh axis runs over, the one named last changes fastest.
Arguments:
- amplitudes: float32 [64, 2, 640], P('row', None, 'col'), may hold values from -6 to 6
- integrals: float32 [2, 640, 640, 640], P(None, 'col', 'row'), may hold values from -0.5 to 0.5
- virt_irrep: int32 [640], replicated, may hold values from 0 to 7
- pair_irrep: int32 [64], replicated, may hold values from 0 to 7
- tile_mask: int32 [8, 8], replicated, may hold values 0 or 1
Outputs:
- residual: float32 [64, 640, 640], P('col', 'row')
The draws below stay inside these ranges and needn't reach their ends.
All inputs are finite; a program needn't handle non-finite values.
Results may differ from the reference program's by a relative error of at most 0.000071.
Values sent between devices are 32-bit elements; how exact they have to be, the bound alone decides.
A program may use at most 192 MiB of HBM per device.

```python
import jax
import jax.numpy as jnp
from jax import lax

V = 640
NIRREP = 8
CS = 2
P_SIZE = 64


def touch_ends(array, key, least, high):
    index_at = [jax.random.randint(jax.random.fold_in(key, axis), (), 0, length) for axis, length in enumerate(array.shape)]
    longest = array.shape.index(max(array.shape))
    beside = index_at[:longest] + [(index_at[longest] + 1) % array.shape[longest]] + index_at[longest + 1:]
    return array.at[tuple(index_at)].set(least).at[tuple(beside)].set(high)


def level_of(stream_key, dims, shards, least, top_value):
    def one(dim, parts):
        steps = jax.random.uniform(jax.random.fold_in(jax.random.fold_in(stream_key, 6), dim), (parts,), jnp.float32, least / len(shards), top_value / len(shards))
        return jnp.repeat(jnp.exp(steps), dims[dim] // parts).reshape((-1,) + (1,) * (len(dims) - dim - 1))

    loudness = one(*shards[0])
    for cut in shards[1:]:
        loudness = loudness * one(*cut)
    return loudness


def noise(rng, shape, width, reach, split=(), kind=jnp.bfloat16):
    loudness = level_of(rng, shape, split, -0.22, 0.18) if split else 1.0
    array = jax.random.normal(rng, shape, jnp.float32) * width * loudness
    return jnp.minimum(jnp.maximum(array, -reach), reach).astype(kind)


def setup_inputs(seed: int = 0) -> dict:
    streams_of = jax.random.split(jax.random.key(seed), 6)
    return {
        "amplitudes": noise(streams_of[0], (P_SIZE, CS, V), 1.0, 6.0, ((0, 8), (2, 4)), jnp.float32),
        "integrals": noise(streams_of[1], (CS, V, V, V), (CS * V // 10) ** -0.5, 0.5, ((1, 4), (2, 8)), jnp.float32),
        "virt_irrep": touch_ends(jax.random.randint(streams_of[2], (V,), 0, NIRREP), jax.random.fold_in(streams_of[2], 1), 0, NIRREP - 1).astype(jnp.int32),
        "pair_irrep": touch_ends(jax.random.randint(streams_of[3], (P_SIZE,), 0, NIRREP), jax.random.fold_in(streams_of[3], 1), 0, NIRREP - 1).astype(jnp.int32),
        "tile_mask": touch_ends((jax.random.randint(streams_of[4], (NIRREP, NIRREP), 0, 4) < 3).astype(jnp.int32), jax.random.fold_in(streams_of[4], 1), 0, 1),
    }


def reference(amplitudes, integrals, virt_irrep, pair_irrep, tile_mask):
    c_labels = virt_irrep[:CS]
    screen = tile_mask.astype(amplitudes.dtype)[c_labels[:, None], virt_irrep[None, :]]
    allowed = jnp.bitwise_xor(c_labels[:, None], virt_irrep[None, :])[None, :, :] == pair_irrep[:, None, None]
    masked = amplitudes * screen[None, :, :] * allowed.astype(amplitudes.dtype)
    ladder = jnp.dot(masked.reshape(P_SIZE, CS * V), integrals.reshape(CS * V, V * V), precision=lax.Precision.HIGHEST, preferred_element_type=jnp.float32).reshape(P_SIZE, V, V)
    mirrored = ladder - jnp.transpose(ladder, (0, 2, 1))
    kept_mask = jnp.bitwise_xor(virt_irrep[:, None], virt_irrep[None, :])[None, :, :] == pair_irrep[:, None, None]
    return mirrored * kept_mask.astype(mirrored.dtype)
```

```python
import functools

import jax
import jax.numpy as jnp
from jax import lax
from jax.experimental import pallas as pl
from jax.experimental.pallas import tpu as pltpu
from jax.sharding import PartitionSpec as P

MESH = pl.DeviceIdType.MESH
F32 = jnp.float32
BF16 = jnp.bfloat16


def split(x):
    high = x.astype(BF16)
    return high, (x - high.astype(F32)).astype(BF16)


def mm(a, b):
    return jnp.dot(a, b, preferred_element_type=F32)


def mm3(a, b):
    return jnp.dot(a, b, precision=lax.Precision.HIGHEST, preferred_element_type=F32)


def exchange(blocks, axis):
    return lax.all_to_all(blocks, axis, split_axis=0, concat_axis=0, tiled=True)


def mask_slab(amps, c_labels, d_labels, pair_irrep, tile_mask):
    labels_range = jnp.arange(tile_mask.shape[0], dtype=jnp.int32)
    c_onehot = (c_labels[:, None] == labels_range[None, :]).astype(F32)
    d_onehot = (d_labels[:, None] == labels_range[None, :]).astype(F32)
    by_c = jnp.sum(c_onehot[:, :, None] * tile_mask.astype(F32)[None], axis=1)
    screen = jnp.sum(by_c[:, None, :] * d_onehot[None], axis=2)
    allowed = (
        jnp.bitwise_xor(c_labels[:, None], d_labels[None, :])[None, :, :]
        == pair_irrep[:, None, None]
    )
    return amps * screen[None, :, :] * allowed.astype(F32)


def gather_kernel(n, x_ref, o_ref, local_sem, send_sem, recv_sem):
    me = lax.axis_index("row")
    rows = x_ref.shape[0]
    barrier = pltpu.get_barrier_semaphore()
    for off in range(1, n):
        pl.semaphore_signal(barrier, inc=1, device_id={"row": lax.rem(me + off, n)}, device_id_type=MESH)
    pl.semaphore_wait(barrier, n - 1)
    here = pl.ds(pl.multiple_of(me * rows, 8), rows)
    copies = []
    for off in range(1, n):
        copies.append(
            pltpu.make_async_remote_copy(
                src_ref=x_ref,
                dst_ref=o_ref.at[here],
                send_sem=send_sem.at[off - 1],
                recv_sem=recv_sem.at[off - 1],
                device_id={"row": lax.rem(me + off, n)},
                device_id_type=MESH,
            )
        )
        copies[-1].start()
    own = pltpu.make_async_copy(x_ref, o_ref.at[here], local_sem)
    own.start()
    own.wait()
    for copy in copies:
        copy.wait()


def gather_rows(x, n):
    rows, width = x.shape
    return pl.pallas_call(
        functools.partial(gather_kernel, n),
        out_shape=jax.ShapeDtypeStruct((n * rows, width), x.dtype),
        in_specs=[pl.BlockSpec(memory_space=pltpu.VMEM)],
        out_specs=pl.BlockSpec(memory_space=pltpu.VMEM),
        scratch_shapes=[
            pltpu.SemaphoreType.DMA,
            pltpu.SemaphoreType.DMA((n - 1,)),
            pltpu.SemaphoreType.DMA((n - 1,)),
        ],
        compiler_params=pltpu.CompilerParams(collective_id=0, has_side_effects=True),
    )(x)


def ladder_kernel(
    nrow, ncol, steps, cap, chunks,
    label_ref, m_ref, xb_ref, xo_ref, al_ref, f_ref, ft_ref, fl_ref, u_ref, *refs,
):
    w_refs = refs[:chunks]
    (
        o_ref, d_s, e_s, er_s, l_s, y_s, ys_s, yr_s, zt_s, own_sem, es_sem, er_sem, ys_sem, yr_sem,
    ) = refs[chunks:]
    step = pl.program_id(0)
    row, col = lax.axis_index("row"), lax.axis_index("col")
    depth, tile, part = w_refs[0].shape
    width = part * chunks
    pairs = xb_ref.shape[0]
    own = xo_ref.shape[0]
    aw = tile * steps
    lanes = f_ref.shape[1]

    def e_copy(at, off):
        peer = lax.rem(col + off, ncol)
        rows = pl.ds(pl.multiple_of(at * tile, 8), tile)
        return pltpu.make_async_remote_copy(
            src_ref=e_s.at[rows, pl.ds(pl.multiple_of(peer * own, 8), own)],
            dst_ref=er_s.at[off - 1, rows],
            send_sem=es_sem.at[at, off - 1],
            recv_sem=er_sem.at[at, off - 1],
            device_id={"col": peer},
            device_id_type=MESH,
        )

    def y_copy(off):
        peer = lax.rem(row + off, nrow)
        return pltpu.make_async_remote_copy(
            src_ref=ys_s.at[pl.ds(pl.multiple_of(peer * aw, 8), aw)],
            dst_ref=yr_s.at[row, pl.ds(0, aw)],
            send_sem=ys_sem.at[off - 1],
            recv_sem=yr_sem.at[off - 1],
            device_id={"row": peer},
            device_id_type=MESH,
        )

    @pl.when(step == 0)
    def _():
        barrier = pltpu.get_barrier_semaphore()
        for off in range(1, ncol):
            pl.semaphore_signal(barrier, inc=1, device_id={"col": lax.rem(col + off, ncol)}, device_id_type=MESH)
        for off in range(1, nrow):
            pl.semaphore_signal(barrier, inc=1, device_id={"row": lax.rem(row + off, nrow)}, device_id_type=MESH)
        pl.semaphore_wait(barrier, ncol + nrow - 2)

    @pl.when(step > 0)
    def _():
        for off in range(1, ncol):
            e_copy(step - 1, off).start()

    w_flat = [ref.reshape(depth * tile, part) for ref in w_refs]

    m_high, m_low = split(m_ref[...])
    m_both = jnp.concatenate([m_high, m_low], axis=0)

    def one_row(i, carry):
        high, low = split(jnp.concatenate([x[pl.ds(i, depth, stride=tile), :] for x in w_flat], axis=1))
        both = mm(m_both, high)
        total = both[:pairs] + both[pairs:] + mm(m_high, low)
        kept = jnp.where(xb_ref[...] == label_ref[step * tile + i], total, 0.0)
        d_s[pl.ds(pl.multiple_of(i * pairs, 8), pairs), :] = kept
        return carry

    for i in range(tile):
        one_row(i, 0)
    high, low = split(d_s[...])
    folded = mm(high, f_ref[...]) + mm(low, f_ref[...])
    e_s[pl.ds(pl.multiple_of(step * tile, 8), tile)] = folded.reshape(tile, pairs, lanes)

    @pl.when(step == steps - 1)
    def _():
        for off in range(1, ncol):
            e_copy(step, off).start()
        def wait_tile(at, carry):
            for off in range(1, ncol):
                e_copy(at, off).wait()
            return carry

        lax.fori_loop(0, steps, wait_tile, 0)
        mine = pl.ds(pl.multiple_of(col * own, 8), own)
        total = e_s[:, mine, :]
        for off in range(1, ncol):
            total = total + er_s[off - 1]
        er_s[0] = total
        t_flat = er_s.at[0].reshape(aw * own, lanes)

        def expand(p, carry):
            high, low = split(t_flat[pl.ds(p, aw, stride=own), :])
            wide = mm(high, ft_ref[...]) + mm(low, ft_ref[...])
            kept = jnp.where(xo_ref[pl.ds(p, 1), :] == al_ref[...], wide, 0.0)
            l_s[pl.ds(pl.multiple_of(p * aw, 8), aw), :] = kept
            high, low = split(kept)
            y_s[pl.ds(pl.multiple_of(p * cap, 8), cap), :] = mm(fl_ref[...], high) + mm(fl_ref[...], low)
            return carry

        lax.fori_loop(0, own, expand, 0)
        ys_s[...] = y_s[...].T
        for off in range(1, nrow):
            y_copy(off).start()
        local = pltpu.make_async_copy(
            ys_s.at[pl.ds(pl.multiple_of(row * aw, 8), aw)], yr_s.at[row, pl.ds(0, aw)], own_sem
        )
        local.start()
        local.wait()
        for off in range(1, nrow):
            y_copy(off).wait()
        for r in range(nrow):
            zt_s[:, r * cap:(r + 1) * cap, :] = yr_s[r].T.reshape(own, cap, yr_s.shape[1])

        def finish(p, carry):
            high, low = split(zt_s[p].T)
            wide = mm(high, u_ref[...]) + mm(low, u_ref[...])
            kept = jnp.where(xo_ref[pl.ds(p, 1), :] == al_ref[...], wide[:aw], 0.0)
            o_ref[p] = l_s[pl.ds(pl.multiple_of(p * aw, 8), aw), :] - kept
            return carry

        lax.fori_loop(0, own, finish, 0)


def sparse_path(masked, w, virt_irrep, pair_irrep, rank, block_rank, a_labels, pair_labels, nrow, ncol, cap, lanes):
    depth, aw, width = w.shape
    pairs = pair_irrep.shape[0]
    own = pairs // ncol
    tile = 8
    chunks = width // lanes
    steps = aw // tile
    pad = -(-aw // 128) * 128
    row_index = lax.axis_index("row")
    lane_ids = jnp.arange(lanes, dtype=jnp.int32)
    fold = (rank[:, None] == lane_ids[None, :]).astype(BF16)
    unfold = (lane_ids[:, None] == rank[None, :]).astype(BF16)
    own_rank = lax.dynamic_slice_in_dim(block_rank, row_index * aw, aw)
    fold_rows = (jnp.arange(cap, dtype=jnp.int32)[:, None] == own_rank[None, :]).astype(BF16)
    slot = (jnp.arange(width, dtype=jnp.int32) // aw) * cap + block_rank
    unfold_rows = (jnp.arange(nrow * cap, dtype=jnp.int32)[:, None] == slot[None, :]).astype(BF16)
    whole = pl.BlockSpec(memory_space=pltpu.VMEM)
    return pl.pallas_call(
        functools.partial(ladder_kernel, nrow, ncol, steps, cap, chunks),
        grid=(steps,),
        out_shape=jax.ShapeDtypeStruct((own, aw, width), F32),
        in_specs=[
            pl.BlockSpec(memory_space=pltpu.SMEM),
        ] + [whole] * 8 + [
            pl.BlockSpec((depth, tile, width // chunks), lambda i, at=at: (0, i, at)) for at in range(chunks)
        ],
        out_specs=whole,
        scratch_shapes=[
            pltpu.VMEM((tile * pairs, width), F32),
            pltpu.VMEM((aw, pairs, lanes), F32),
            pltpu.VMEM((ncol - 1, aw, own, lanes), F32),
            pltpu.VMEM((own * aw, width), F32),
            pltpu.VMEM((own * cap, width), F32),
            pltpu.VMEM((width, own * cap), F32),
            pltpu.VMEM((nrow, pad, own * cap), F32),
            pltpu.VMEM((own, nrow * cap, pad), F32),
            pltpu.SemaphoreType.DMA,
            pltpu.SemaphoreType.DMA((steps, ncol - 1)),
            pltpu.SemaphoreType.DMA((steps, ncol - 1)),
            pltpu.SemaphoreType.DMA((nrow - 1,)),
            pltpu.SemaphoreType.DMA((nrow - 1,)),
        ],
        compiler_params=pltpu.CompilerParams(
            collective_id=1, has_side_effects=True, vmem_limit_bytes=60 * 1024 * 1024
        ),
    )(
        a_labels,
        masked,
        jnp.bitwise_xor(virt_irrep[None, :], pair_irrep[:, None]),
        jnp.bitwise_xor(virt_irrep[None, :], pair_labels[:, None]),
        jnp.broadcast_to(a_labels[:, None], (aw, width)),
        fold,
        unfold,
        fold_rows,
        unfold_rows,
        *([w] * chunks),
    )


def dense_path(masked, w, virt_irrep, a_labels, pair_labels, ncol):
    depth, aw, width = w.shape
    pairs = masked.shape[0]
    own = pairs // ncol
    partial_sums = mm3(masked, w.reshape(depth, aw * width)).reshape(pairs, aw, width)
    owned = jnp.sum(exchange(partial_sums, "col").reshape(ncol, own, aw, width), axis=0)
    swapped = lax.all_to_all(owned, "row", split_axis=2, concat_axis=1, tiled=True)
    mirrored = owned - jnp.transpose(swapped, (0, 2, 1))
    kept = jnp.bitwise_xor(a_labels[:, None], virt_irrep[None, :])[None] == pair_labels[:, None, None]
    return mirrored * kept.astype(F32)


def local(nrow, ncol, amplitudes, integrals, virt_irrep, pair_irrep, tile_mask):
    own_p, slab, d_width = amplitudes.shape
    aw, width = integrals.shape[2:]
    depth = slab * d_width
    row_index = lax.axis_index("row")
    col_index = lax.axis_index("col")
    w = integrals.reshape(depth, aw, width)
    gathered = gather_rows(amplitudes.reshape(own_p, depth), nrow).reshape(-1, slab, d_width)
    pairs = gathered.shape[0]
    own = pairs // ncol
    c_labels = virt_irrep[:slab]
    d_labels = lax.dynamic_slice_in_dim(virt_irrep, col_index * d_width, d_width)
    masked = mask_slab(gathered, c_labels, d_labels, pair_irrep, tile_mask).reshape(pairs, depth)
    a_labels = lax.dynamic_slice_in_dim(virt_irrep, row_index * aw, aw)
    pair_labels = lax.dynamic_slice_in_dim(pair_irrep, col_index * own, own)
    if aw % 8 or own % 8:
        return dense_path(masked, w, virt_irrep, a_labels, pair_labels, ncol)
    lanes = 128
    cap = min(-(-3 * aw // (10 * 8)) * 8, aw)
    index = jnp.arange(width, dtype=jnp.int32)
    same = (virt_irrep[:, None] == virt_irrep[None, :]) & (index[None, :] < index[:, None])
    rank = jnp.sum(same.astype(jnp.int32), axis=1)
    near = same & (index[:, None] // aw == index[None, :] // aw)
    block_rank = jnp.sum(near.astype(jnp.int32), axis=1)
    fits = (jnp.max(rank) < lanes) & (jnp.max(block_rank) < cap)
    return lax.cond(
        fits,
        lambda m, x: sparse_path(
            m, x, virt_irrep, pair_irrep, rank, block_rank, a_labels, pair_labels, nrow, ncol, cap, lanes
        ),
        lambda m, x: dense_path(m, x, virt_irrep, a_labels, pair_labels, ncol),
        masked,
        w,
    )


def solution(mesh):
    in_specs = (P("row", None, "col"), P(None, "col", "row", None), P(), P(), P())
    out_specs = P("col", "row", None)
    body = functools.partial(local, mesh.shape["row"], mesh.shape["col"])
    return jax.shard_map(body, mesh=mesh, in_specs=in_specs, out_specs=out_specs, check_vma=False)
```
